32 devices in a mesh: ctx: 8 (over y, x, core), head: 4 (over z).
Axes of the slice: x: 2, y: 2, z: 4, core: 2. Of those that a mesh axis runs over, the one named last changes fastest.
Arguments:
- queries: bfloat16 [4096, 4096], P(('ctx', 'head')), may hold values from -34 to 34
- key_rows: bfloat16 [4096, 2048], P(('ctx', 'head')), may hold values from -34 to 34
- value_rows: bfloat16 [4096, 2048], P(('ctx', 'head')), may hold values from -6 to 6
- out_grad: bfloat16 [4096, 4096], P(('ctx', 'head')), may hold values from -6 to 6
Outputs:
- query_grad: bfloat16 [4096, 4096], P(('ctx', 'head'))
- key_grad: bfloat16 [4096, 2048], P(('ctx', 'head'))
- value_grad: bfloat16 [4096, 2048], P(('ctx', 'head'))
The draws below stay inside these ranges and needn't reach their ends.
All inputs are finite; a program needn't handle non-finite values.
Results may differ from the reference program's by a relative error of at most 0.0072.
Values may be sent and summed in bfloat16 or wider, within the bound.
No kernel may reach another device: no remote copies, remote signals or barrier semaphores. Data moves between devices by JAX's collectives and lax.ppermute only.
A program may use at most 128 MiB of HBM per device.

```python
import jax
import jax.numpy as jnp
from jax import lax

HEAD_DIM = 128
Q_HEADS = 32
KV_HEADS = 16
WINDOW = 1024
TOK_CTX = 512
SEQ = 4096


def drawn_rows(key):
    base_keys = jnp.clip(jax.random.normal(jax.random.fold_in(key, 11), (SEQ, KV_HEADS, HEAD_DIM), jnp.float32), -6.0, 6.0)
    return base_keys


def draw_key_rows(key, part):
    base_keys = drawn_rows(key)
    result = base_keys
    return result.reshape(SEQ, KV_HEADS * HEAD_DIM).astype(jnp.bfloat16)


def draw_queries(key, part):
    result = jnp.clip(jax.random.normal(jax.random.fold_in(key, 13), (SEQ, Q_HEADS, HEAD_DIM), jnp.float32), -6.0, 6.0)
    return result.reshape(SEQ, Q_HEADS * HEAD_DIM).astype(jnp.bfloat16)


def block_levels(own_key, extent, cuts, low, high):
    factor_of, own = 1.0, jax.random.fold_in(own_key, 6)
    for position, blocks in cuts:
        heights = jnp.exp(jax.random.uniform(jax.random.fold_in(own, position), (blocks,), jnp.float32, low / len(cuts), high / len(cuts)))
        factor_of = factor_of * jnp.repeat(heights, extent[position] // blocks).reshape([-1 if axis == position else 1 for axis in range(len(extent))])
    return factor_of


def bell_draw(rng, shape, scale, bound, shards=(), kind=jnp.bfloat16):
    gain = block_levels(rng, shape, shards, -0.22, 0.18) if shards else 1.0
    drawn = jax.random.normal(rng, shape, jnp.float32) * scale * gain
    return jnp.minimum(jnp.maximum(drawn, -bound), bound).astype(kind)


def setup_inputs(seed: int = 0) -> dict:
    key_list = jax.random.split(jax.random.key(seed), 5)
    return {
        "queries": draw_queries(jax.random.fold_in(key_list[4], 71), 0),
        "key_rows": draw_key_rows(jax.random.fold_in(key_list[4], 71), 0),
        "value_rows": bell_draw(key_list[2], (SEQ, KV_HEADS * HEAD_DIM), 1.0, 6.0, ((0, 32),)),
        "out_grad": bell_draw(key_list[3], (SEQ, Q_HEADS * HEAD_DIM), 1.0, 6.0, ((0, 32),)),
    }


score_scale = 168.0 ** -0.5


def reference(queries, key_rows, value_rows, out_grad):
    groups = Q_HEADS // KV_HEADS
    key_count = WINDOW + TOK_CTX
    query_all = queries.reshape(SEQ, Q_HEADS, HEAD_DIM)
    grad_all = out_grad.reshape(SEQ, Q_HEADS, HEAD_DIM)
    key_pad = jnp.concatenate([jnp.zeros((WINDOW, KV_HEADS, HEAD_DIM), key_rows.dtype), key_rows.reshape(SEQ, KV_HEADS, HEAD_DIM)], axis=0)
    value_pad = jnp.concatenate([jnp.zeros((WINDOW, KV_HEADS, HEAD_DIM), value_rows.dtype), value_rows.reshape(SEQ, KV_HEADS, HEAD_DIM)], axis=0)
    row_ids = jnp.arange(TOK_CTX, dtype=jnp.int32)[:, None]
    col_ids = jnp.arange(key_count, dtype=jnp.int32)[None, :]

    def block_step(carried, block_number):
        key_accum, value_accum = carried
        first_row = (block_number * TOK_CTX).astype(jnp.int32)
        query_block = lax.dynamic_slice_in_dim(query_all, first_row, TOK_CTX, 0).astype(jnp.float32)
        grad_block = lax.dynamic_slice_in_dim(grad_all, first_row, TOK_CTX, 0).astype(jnp.float32)
        key_block = jnp.repeat(lax.dynamic_slice_in_dim(key_pad, first_row, key_count, 0).astype(jnp.float32), groups, axis=1)
        value_block = jnp.repeat(lax.dynamic_slice_in_dim(value_pad, first_row, key_count, 0).astype(jnp.float32), groups, axis=1)
        scores = score_scale * jnp.einsum("tqd,kqd->qtk", query_block, key_block)
        allowed = (col_ids > row_ids) & (col_ids <= row_ids + WINDOW) & (col_ids >= WINDOW - first_row)
        scores = jnp.where(allowed[None], scores, -1e30)
        row_top = jnp.max(scores, axis=-1, keepdims=True)
        raised = jnp.exp(scores - row_top)
        attention = raised / jnp.sum(raised, axis=-1, keepdims=True)
        d_attention = jnp.einsum("tqd,kqd->qtk", grad_block, value_block)
        center = jnp.sum(attention * d_attention, axis=-1, keepdims=True)
        d_score = lax.optimization_barrier((attention * (d_attention - center)).astype(jnp.bfloat16)).astype(jnp.float32)
        attention_low = lax.optimization_barrier(attention.astype(jnp.bfloat16)).astype(jnp.float32)
        query_part = (score_scale * jnp.einsum("qtk,kqd->tqd", d_score, key_block)).astype(jnp.bfloat16)
        key_part = score_scale * jnp.einsum("qtk,tqd->kqd", d_score, query_block).reshape(key_count, KV_HEADS, groups, HEAD_DIM).sum(axis=2)
        value_part = jnp.einsum("qtk,tqd->kqd", attention_low, grad_block).reshape(key_count, KV_HEADS, groups, HEAD_DIM).sum(axis=2)
        key_accum = lax.dynamic_update_slice_in_dim(key_accum, lax.dynamic_slice_in_dim(key_accum, first_row, key_count, 0) + key_part, first_row, 0)
        value_accum = lax.dynamic_update_slice_in_dim(value_accum, lax.dynamic_slice_in_dim(value_accum, first_row, key_count, 0) + value_part, first_row, 0)
        return (key_accum, value_accum), query_part

    empty_sums = jnp.zeros((WINDOW + SEQ, KV_HEADS, HEAD_DIM), jnp.float32)
    (key_accum, value_accum), query_parts = lax.scan(block_step, (empty_sums, empty_sums), jnp.arange(SEQ // TOK_CTX, dtype=jnp.int32))
    query_grad = query_parts.reshape(SEQ, Q_HEADS * HEAD_DIM)
    key_grad = key_accum[WINDOW:].reshape(SEQ, KV_HEADS * HEAD_DIM).astype(jnp.bfloat16)
    value_grad = value_accum[WINDOW:].reshape(SEQ, KV_HEADS * HEAD_DIM).astype(jnp.bfloat16)
    return (query_grad, key_grad, value_grad)
```

```python
import functools

import jax
import jax.numpy as jnp
from jax import lax
from jax.experimental import pallas as pl
from jax.experimental.pallas import tpu as pltpu
from jax.sharding import PartitionSpec as P


HEAD_DIM = 128
Q_HEADS = 32
KV_HEADS = 16
WINDOW = 1024
GROUPS = Q_HEADS // KV_HEADS
Q_COLS = GROUPS * HEAD_DIM
TILE = 128

score_scale = 168.0 ** (-0.5)
LOG2_E = 1.4426950408889634


def vmem():
    return pl.BlockSpec(memory_space=pltpu.VMEM)


def smem():
    return pl.BlockSpec(memory_space=pltpu.SMEM)


def moved_bytes(arrays):
    return sum(a.size * a.dtype.itemsize for a in arrays)


def local_call(body, outs, args, flops=0, transcendentals=0, scratch=()):
    return pl.pallas_call(
        body,
        out_shape=outs,
        in_specs=[smem()] + [vmem()] * (len(args) - 1),
        out_specs=[vmem()] * len(outs),
        scratch_shapes=list(scratch),
        cost_estimate=pl.CostEstimate(
            flops=flops,
            transcendentals=transcendentals,
            bytes_accessed=moved_bytes(list(args[1:]) + list(outs)),
        ),
    )(*args)


def across(shard, parts, step):
    return lax.ppermute(shard, "head", [(i, i ^ step) for i in range(parts)])


def shifted(shard, by):
    count = lax.axis_size("ctx")
    pairs = [(i, i + by) for i in range(count) if 0 <= i + by < count]
    return lax.ppermute(shard, "ctx", pairs)


def pack_two(parts, width, chunks, place, left, right, *outs):
    for step in range(parts):
        partner = jnp.bitwise_xor(place[0], step)
        for chunk in range(chunks):
            out = outs[step * chunks + chunk]
            start = pl.multiple_of((partner * chunks + chunk) * width, width)
            out[:, 0:width] = left[:, pl.ds(start, width)]
            out[:, width : 2 * width] = right[:, pl.ds(start, width)]


def join_rows(parts, chunks, place, *refs):
    outs = refs[parts:]
    rows = refs[0].shape[0]
    for step in range(parts):
        partner = jnp.bitwise_xor(place[0], step)
        at = pl.ds(pl.multiple_of(partner * rows, rows), rows)
        for chunk in range(chunks):
            for side in range(2):
                start = (side * chunks + chunk) * HEAD_DIM
                outs[chunk][at, side * HEAD_DIM : (side + 1) * HEAD_DIM] = refs[step][
                    :, start : start + HEAD_DIM
                ]


def attend(parts, place, far, near, own, *refs):
    pieces = refs[:parts]
    dq_out, own_out, near_out, far_out = refs[parts : parts + 4]
    q_rows, g_rows, keys, values, keys_t, score, d_att, att_low, d_low, dk, dv = refs[parts + 4 :]
    rows = pieces[0].shape[0]
    block = rows * parts
    span = score.shape[0]
    tiles = span // TILE
    for step in range(parts):
        partner = jnp.bitwise_xor(place[0], step)
        at = pl.ds(pl.multiple_of(partner * rows, rows), rows)
        q_rows[at, :] = pieces[step][:, 0:Q_COLS]
        g_rows[at, :] = pieces[step][:, Q_COLS : 2 * Q_COLS]
    for i, kv in enumerate((far, near, own)):
        there = slice(i * block, (i + 1) * block)
        keys[there, :] = kv[:, 0:HEAD_DIM]
        values[there, :] = kv[:, HEAD_DIM : 2 * HEAD_DIM]
        keys_t[:, there] = kv[:, 0:HEAD_DIM].T
    dk[...] = jnp.zeros_like(dk)
    dv[...] = jnp.zeros_like(dv)
    first_key = WINDOW - place[1] * block
    lanes = GROUPS * TILE
    key_id = lax.broadcasted_iota(jnp.int32, (TILE, lanes), 0)
    row_id = jnp.bitwise_and(lax.broadcasted_iota(jnp.int32, (TILE, lanes), 1), TILE - 1)
    lower = key_id <= row_id
    across_cols = (((1,), (1,)), ((), ()))
    exponent = jnp.float32(score_scale * LOG2_E)

    def fold(x):
        return x.reshape(TILE // 8, 8, lanes)

    for row_block in range(block // TILE):
        base = row_block * TILE
        these = slice(base, base + TILE)
        q_two = jnp.concatenate(
            [q_rows[these, g * HEAD_DIM : (g + 1) * HEAD_DIM] for g in range(GROUPS)], axis=0
        )
        g_two = jnp.concatenate(
            [g_rows[these, g * HEAD_DIM : (g + 1) * HEAD_DIM] for g in range(GROUPS)], axis=0
        )
        top = jnp.full((8, lanes), -1e30, jnp.float32)
        for t in range(tiles):
            s = lax.dot_general(
                keys[base + t * TILE : base + (t + 1) * TILE, :],
                q_two,
                across_cols,
                preferred_element_type=jnp.float32,
            )
            if t == 0:
                s = jnp.where(lower, -1e30, s)
            if t == tiles - 1:
                s = jnp.where(lower, s, -1e30)
            score[t * TILE : (t + 1) * TILE, :] = s
            gone = jnp.where(base + t * TILE < first_key, -1e30, 0.0)
            top = jnp.maximum(top, jnp.max(fold(s), axis=0) + gone)
        top = jnp.max(top, axis=0, keepdims=True)
        total = jnp.zeros((8, lanes), jnp.float32)
        inner = jnp.zeros((8, lanes), jnp.float32)
        for t in range(tiles):
            here = slice(t * TILE, (t + 1) * TILE)
            level = top + jnp.where(base + t * TILE < first_key, 1e30, 0.0)
            p = jnp.exp2((score[here, :] - level) * exponent)
            score[here, :] = p
            total = total + jnp.sum(fold(p), axis=0)
            d = lax.dot_general(
                values[base + t * TILE : base + (t + 1) * TILE, :],
                g_two,
                across_cols,
                preferred_element_type=jnp.float32,
            )
            d_att[here, :] = d
            inner = inner + jnp.sum(fold(p * d), axis=0)
        inverse = 1.0 / jnp.sum(total, axis=0, keepdims=True)
        center = jnp.sum(inner, axis=0, keepdims=True) * inverse
        for t in range(tiles):
            here = slice(t * TILE, (t + 1) * TILE)
            att = score[here, :] * inverse
            att_low[here, :] = att.astype(jnp.bfloat16)
            d_low[here, :] = (att * (d_att[here, :] - center)).astype(jnp.bfloat16)
        there = slice(base, base + span)
        dv[there, :] += jnp.dot(att_low[...], g_two, preferred_element_type=jnp.float32)
        dk[there, :] += jnp.dot(d_low[...], q_two, preferred_element_type=jnp.float32)
        dq_t = jnp.dot(keys_t[:, there], d_low[...], preferred_element_type=jnp.float32)
        dq = (dq_t * score_scale).T.astype(jnp.bfloat16)
        for g in range(GROUPS):
            dq_out[these, g * HEAD_DIM : (g + 1) * HEAD_DIM] = dq[g * TILE : (g + 1) * TILE, :]
    for out, start in ((far_out, 0), (near_out, block), (own_out, 2 * block)):
        out[:, 0:HEAD_DIM] = (dk[start : start + block, :] * score_scale).astype(out.dtype)
        out[:, HEAD_DIM : 2 * HEAD_DIM] = dv[start : start + block, :].astype(out.dtype)


def add_up(parts, place, dq, own, near, far, *outs):
    rows = outs[0].shape[0]
    for step in range(parts):
        partner = jnp.bitwise_xor(place[0], step)
        at = pl.ds(pl.multiple_of(partner * rows, rows), rows)
        outs[step][:, 0:Q_COLS] = dq[at, :]
        total = own[at, :] + near[at, :].astype(jnp.float32) + far[at, :].astype(jnp.float32)
        outs[step][:, Q_COLS : Q_COLS + 2 * HEAD_DIM] = total.astype(jnp.bfloat16)


def unpack(parts, chunks, place, *refs):
    pieces = refs[: parts * chunks]
    dq, dk, dv = refs[parts * chunks :]
    for step in range(parts):
        partner = jnp.bitwise_xor(place[0], step)
        for chunk in range(chunks):
            piece = pieces[step * chunks + chunk]
            slot = partner * chunks + chunk
            dq[:, pl.ds(pl.multiple_of(slot * Q_COLS, Q_COLS), Q_COLS)] = piece[:, 0:Q_COLS]
            at = pl.ds(pl.multiple_of(slot * HEAD_DIM, HEAD_DIM), HEAD_DIM)
            dk[:, at] = piece[:, Q_COLS : Q_COLS + HEAD_DIM]
            dv[:, at] = piece[:, Q_COLS + HEAD_DIM : Q_COLS + 2 * HEAD_DIM]


def shards(queries, key_rows, value_rows, out_grad):
    parts = lax.axis_size("head")
    rows = queries.shape[0]
    block = rows * parts
    chunks = KV_HEADS // parts
    key_count = WINDOW + block
    span = WINDOW + TILE
    low, wide = jnp.bfloat16, jnp.float32
    place = jnp.stack([lax.axis_index("head"), lax.axis_index("ctx")]).astype(jnp.int32)
    kv_width = chunks * HEAD_DIM

    kv_piece = jax.ShapeDtypeStruct((rows, 2 * kv_width), low)
    kv_pieces = local_call(
        functools.partial(pack_two, parts, kv_width, 1),
        [kv_piece] * parts,
        (place, key_rows, value_rows),
    )
    kv_pieces = [kv_pieces[0]] + [across(kv_pieces[s], parts, s) for s in range(1, parts)]
    q_piece = jax.ShapeDtypeStruct((rows, 2 * Q_COLS), low)
    q_pieces = local_call(
        functools.partial(pack_two, parts, Q_COLS, chunks),
        [q_piece] * (parts * chunks),
        (place, queries, out_grad),
    )
    arrived = {}
    for chunk in range(chunks):
        for step in range(parts):
            piece = q_pieces[step * chunks + chunk]
            if step:
                piece = across(piece, parts, step)
            arrived[chunk, step] = piece

    half = jax.ShapeDtypeStruct((block, 2 * HEAD_DIM), low)
    kv_own = local_call(
        functools.partial(join_rows, parts, chunks), [half] * chunks, (place, *kv_pieces)
    )
    kv_near = [shifted(kv_own[c], 1) for c in range(chunks)]
    kv_far = [shifted(kv_own[c], 2) for c in range(chunks)]

    full = jax.ShapeDtypeStruct((block, 2 * HEAD_DIM), wide)
    lanes = GROUPS * TILE
    pairs = block * span * GROUPS
    back = {}
    for chunk in range(chunks):
        pieces = [arrived[chunk, step] for step in range(parts)]
        sources = [kv_far[chunk], kv_near[chunk], kv_own[chunk]]
        outs = [half, full, half, half]
        call = functools.partial(
            local_call,
            functools.partial(attend, parts),
            outs,
            flops=10 * pairs * HEAD_DIM,
            transcendentals=pairs,
            scratch=[
                pltpu.VMEM((block, Q_COLS), low),
                pltpu.VMEM((block, Q_COLS), low),
                pltpu.VMEM((key_count, HEAD_DIM), low),
                pltpu.VMEM((key_count, HEAD_DIM), low),
                pltpu.VMEM((HEAD_DIM, key_count), low),
                pltpu.VMEM((span, lanes), wide),
                pltpu.VMEM((span, lanes), wide),
                pltpu.VMEM((span, lanes), low),
                pltpu.VMEM((span, lanes), low),
                pltpu.VMEM((key_count, HEAD_DIM), wide),
                pltpu.VMEM((key_count, HEAD_DIM), wide),
            ],
        )
        dq, own, near, far = call((place, *sources, *pieces))
        near = shifted(near, -1)
        far = shifted(far, -2)
        sent = local_call(
            functools.partial(add_up, parts), [q_piece] * parts, (place, dq, own, near, far)
        )
        for step in range(parts):
            piece = sent[step]
            if step:
                piece = across(piece, parts, step)
            back[step * chunks + chunk] = piece
    return tuple(
        local_call(
            functools.partial(unpack, parts, chunks),
            [
                jax.ShapeDtypeStruct(queries.shape, low),
                jax.ShapeDtypeStruct(key_rows.shape, low),
                jax.ShapeDtypeStruct(value_rows.shape, low),
            ],
            (place, *[back[i] for i in range(parts * chunks)]),
        )
    )


def solution(mesh):
    spec = P(("ctx", "head"), None)
    return jax.shard_map(
        shards,
        mesh=mesh,
        in_specs=(spec, spec, spec, spec),
        out_specs=(spec, spec, spec),
        check_vma=False,
    )
```

```python
import functools

import jax
import jax.numpy as jnp
from jax import lax
from jax.experimental import pallas as pl
from jax.experimental.pallas import tpu as pltpu
from jax.sharding import PartitionSpec as P


HEAD_DIM = 128
Q_HEADS = 32
KV_HEADS = 16
WINDOW = 1024
GROUPS = Q_HEADS // KV_HEADS
Q_COLS = GROUPS * HEAD_DIM
TILE = 128

score_scale = 168.0 ** (-0.5)
LOG2_E = 1.4426950408889634


def vmem():
    return pl.BlockSpec(memory_space=pltpu.VMEM)


def smem():
    return pl.BlockSpec(memory_space=pltpu.SMEM)


def moved_bytes(arrays):
    return sum(a.size * a.dtype.itemsize for a in arrays)


def local_call(body, outs, args, flops=0, transcendentals=0, scratch=()):
    return pl.pallas_call(
        body,
        out_shape=outs,
        in_specs=[smem()] + [vmem()] * (len(args) - 1),
        out_specs=[vmem()] * len(outs),
        scratch_shapes=list(scratch),
        cost_estimate=pl.CostEstimate(
            flops=flops,
            transcendentals=transcendentals,
            bytes_accessed=moved_bytes(list(args[1:]) + list(outs)),
        ),
    )(*args)


def sent_to(place, step, parts):
    if parts == 4 and step in (1, 3):
        return lax.rem(2 * place + 1 if step == 1 else 3 * place + 2, 5)
    if parts == 4 and step == 2:
        step = 3
    return jnp.bitwise_xor(place, step)


def came_from(place, step, parts):
    return sent_to(place, (parts - step) % parts if parts == 4 else step, parts)


def across(shard, parts, step):
    if parts == 4:
        moves = list(enumerate({1: (1, 3, 0, 2), 2: (3, 2, 1, 0), 3: (2, 0, 3, 1)}[step]))
    else:
        moves = [(i, i ^ step) for i in range(parts)]
    return lax.ppermute(shard, "head", moves)


def pack_two(parts, width, chunks, place, left, right, *outs):
    for step in range(parts):
        partner = sent_to(place[0], step, parts)
        for chunk in range(chunks):
            out = outs[step * chunks + chunk]
            start = pl.multiple_of((partner * chunks + chunk) * width, width)
            out[:, 0:width] = left[:, pl.ds(start, width)]
            out[:, width : 2 * width] = right[:, pl.ds(start, width)]


def split_rows(parts, pairs, width, place, *refs):
    outs = refs[parts:]
    rows = refs[0].shape[0]
    for step in range(parts):
        partner = came_from(place[0], step, parts)
        at = pl.ds(pl.multiple_of(partner * rows, rows), rows)
        for pair in range(pairs):
            for other in range(len(outs) // pairs):
                core = jnp.bitwise_xor(place[2], other)
                for side in range(2):
                    start = ((side * pairs + pair) * place[3] + core) * width
                    outs[other * pairs + pair][at, side * width : (side + 1) * width] = refs[step][
                        :, pl.ds(pl.multiple_of(start, width), width)
                    ]


def attend(kv_count, q_count, starts, place, *refs):
    kv_refs = refs[:kv_count]
    q_refs = refs[kv_count : kv_count + q_count]
    dq_outs = refs[kv_count + q_count : kv_count + 2 * q_count]
    kv_outs = refs[kv_count + 2 * q_count : 2 * kv_count + 2 * q_count]
    scratch = refs[2 * kv_count + 2 * q_count :]
    q_rows, g_rows, keys, values, keys_t, score, d_att, att_low, d_low, dk, dv, dq_all = scratch
    block = q_refs[0].shape[0]
    span = score.shape[0]
    tiles = span // TILE
    places = [pl.ds(pl.multiple_of(at, TILE), block) for at in starts(place, block)]
    for at, q in zip(places[kv_count:], q_refs):
        q_rows[at, :] = q[:, 0:Q_COLS]
        g_rows[at, :] = q[:, Q_COLS : 2 * Q_COLS]
    for at, kv in zip(places, kv_refs):
        keys[at, :] = kv[:, 0:HEAD_DIM]
        values[at, :] = kv[:, HEAD_DIM : 2 * HEAD_DIM]
        keys_t[:, at] = kv[:, 0:HEAD_DIM].T
    dk[...] = jnp.zeros_like(dk)
    dv[...] = jnp.zeros_like(dv)
    first_key = WINDOW - place[1] * (q_count * block)
    lanes = GROUPS * TILE
    key_id = lax.broadcasted_iota(jnp.int32, (TILE, lanes), 0)
    row_id = jnp.bitwise_and(lax.broadcasted_iota(jnp.int32, (TILE, lanes), 1), TILE - 1)
    lower = key_id <= row_id
    across_cols = (((1,), (1,)), ((), ()))
    exponent = jnp.float32(score_scale * LOG2_E)

    def fold(x):
        return x.reshape(TILE // 8, 8, lanes)

    for row_block in range(q_count * block // TILE):
        base = row_block * TILE
        these = slice(base, base + TILE)
        q_two = jnp.concatenate(
            [q_rows[these, g * HEAD_DIM : (g + 1) * HEAD_DIM] for g in range(GROUPS)], axis=0
        )
        g_two = jnp.concatenate(
            [g_rows[these, g * HEAD_DIM : (g + 1) * HEAD_DIM] for g in range(GROUPS)], axis=0
        )
        there = slice(base, base + span)
        score[...] = lax.dot_general(
            keys[there, :], q_two, across_cols, preferred_element_type=jnp.float32
        )
        d_att[...] = lax.dot_general(
            values[there, :], g_two, across_cols, preferred_element_type=jnp.float32
        )
        score[0:TILE, :] = jnp.where(lower, -1e30, score[0:TILE, :])
        score[span - TILE : span, :] = jnp.where(lower, score[span - TILE : span, :], -1e30)
        top = jnp.full((8, lanes), -1e30, jnp.float32)
        for t in range(tiles):
            s = score[t * TILE : (t + 1) * TILE, :]
            gone = jnp.where(base + t * TILE < first_key, -1e30, 0.0)
            top = jnp.maximum(top, jnp.max(fold(s), axis=0) + gone)
        top = jnp.max(top, axis=0, keepdims=True)
        total = jnp.zeros((8, lanes), jnp.float32)
        inner = jnp.zeros((8, lanes), jnp.float32)
        for t in range(tiles):
            here = slice(t * TILE, (t + 1) * TILE)
            level = top + jnp.where(base + t * TILE < first_key, 1e30, 0.0)
            p = jnp.exp2((score[here, :] - level) * exponent)
            score[here, :] = p
            total = total + jnp.sum(fold(p), axis=0)
            inner = inner + jnp.sum(fold(p * d_att[here, :]), axis=0)
        inverse = 1.0 / jnp.sum(total, axis=0, keepdims=True)
        center = jnp.sum(inner, axis=0, keepdims=True) * inverse
        for t in range(tiles):
            here = slice(t * TILE, (t + 1) * TILE)
            att = score[here, :] * inverse
            att_low[here, :] = att.astype(jnp.bfloat16)
            d_low[here, :] = (att * (d_att[here, :] - center)).astype(jnp.bfloat16)
        dv[there, :] += jnp.dot(att_low[...], g_two, preferred_element_type=jnp.float32)
        dk[there, :] += jnp.dot(d_low[...], q_two, preferred_element_type=jnp.float32)
        dq_t = jnp.dot(keys_t[:, there], d_low[...], preferred_element_type=jnp.float32)
        dq = (dq_t * score_scale).T.astype(jnp.bfloat16)
        for g in range(GROUPS):
            dq_all[these, g * HEAD_DIM : (g + 1) * HEAD_DIM] = dq[g * TILE : (g + 1) * TILE, :]
    for at, out in zip(places[kv_count:], dq_outs):
        out[...] = dq_all[at, :]
    for at, out in zip(places, kv_outs):
        out[:, 0:HEAD_DIM] = (dk[at, :] * score_scale).astype(out.dtype)
        out[:, HEAD_DIM : 2 * HEAD_DIM] = dv[at, :].astype(out.dtype)


def row_starts_single(place, block):
    return [0, block, 2 * block, 0]


def row_starts_pair(place, block):
    here, there = place[2] * block, (1 - place[2]) * block
    return [here, there, 2 * block + here, 2 * block + there, here, there]


def cut_queries(parts, place, kept, given, *outs):
    rows = outs[0].shape[0]
    width = kept.shape[1]
    for step in range(parts):
        at = pl.ds(pl.multiple_of(sent_to(place[0], step, parts) * rows, rows), rows)
        for other, source in enumerate((kept, given)):
            core = jnp.bitwise_xor(place[2], other)
            outs[step][:, pl.ds(pl.multiple_of(core * width, width), width)] = source[at, :]


def cut_keys(parts, place, own, own_far, given, given_far, *outs):
    rows = outs[0].shape[0]
    for step in range(parts):
        at = pl.ds(pl.multiple_of(sent_to(place[0], step, parts) * rows, rows), rows)
        for other, (one, two) in enumerate(((own, own_far), (given, given_far))):
            core = jnp.bitwise_xor(place[2], other)
            total = (one[at, :].astype(jnp.float32) + two[at, :].astype(jnp.float32)).astype(
                jnp.bfloat16
            )
            for side in range(2):
                start = pl.multiple_of((2 * side + core) * HEAD_DIM, HEAD_DIM)
                outs[step][:, pl.ds(start, HEAD_DIM)] = total[
                    :, side * HEAD_DIM : (side + 1) * HEAD_DIM
                ]


def add_up(parts, place, dq, own, near, far, *outs):
    rows = outs[0].shape[0]
    for step in range(parts):
        partner = sent_to(place[0], step, parts)
        at = pl.ds(pl.multiple_of(partner * rows, rows), rows)
        outs[step][:, 0:Q_COLS] = dq[at, :]
        total = own[at, :] + near[at, :].astype(jnp.float32) + far[at, :].astype(jnp.float32)
        outs[parts + step][:, 0 : 2 * HEAD_DIM] = total.astype(jnp.bfloat16)


def unpack(parts, chunks, width, place, *refs):
    pieces = refs[: parts * chunks]
    outs = refs[parts * chunks :]
    for step in range(parts):
        partner = came_from(place[0], step, parts)
        for chunk in range(chunks):
            piece = pieces[step * chunks + chunk]
            start = pl.multiple_of((partner * chunks + chunk) * width, width)
            for i, out in enumerate(outs):
                out[:, pl.ds(start, width)] = piece[:, i * width : (i + 1) * width]


def struct(shape, dtype=jnp.bfloat16):
    return jax.ShapeDtypeStruct(shape, dtype)


def to_partners(pieces, parts):
    return [pieces[0]] + [across(pieces[s], parts, s) for s in range(1, parts)]


def ctx_moved(shard, by, flip):
    count = lax.axis_size("ctx")
    moves = [(i, (i + by) ^ flip) for i in range(count) if 0 <= i + by < count]
    return lax.ppermute(shard, "ctx", moves)


def attend_call(starts, kv, q, kv_dtypes, place):
    block = q[0].shape[0]
    rows, key_count, span = len(q) * block, len(kv) * block, WINDOW + TILE
    lanes = GROUPS * TILE
    pairs = rows * span * GROUPS
    low, wide = jnp.bfloat16, jnp.float32
    outs = [struct((block, Q_COLS))] * len(q) + [
        struct((block, 2 * HEAD_DIM), dtype) for dtype in kv_dtypes
    ]
    result = functools.partial(
        local_call,
        flops=10 * pairs * HEAD_DIM,
        transcendentals=pairs,
        scratch=[
            pltpu.VMEM((rows, Q_COLS), low),
            pltpu.VMEM((rows, Q_COLS), low),
            pltpu.VMEM((key_count, HEAD_DIM), low),
            pltpu.VMEM((key_count, HEAD_DIM), low),
            pltpu.VMEM((HEAD_DIM, key_count), low),
            pltpu.VMEM((span, lanes), wide),
            pltpu.VMEM((span, lanes), wide),
            pltpu.VMEM((span, lanes), low),
            pltpu.VMEM((span, lanes), low),
            pltpu.VMEM((key_count, HEAD_DIM), wide),
            pltpu.VMEM((key_count, HEAD_DIM), wide),
            pltpu.VMEM((rows, Q_COLS), low),
        ],
    )(functools.partial(attend, len(kv), len(q), starts), outs, (place, *kv, *q))
    return result[: len(q)], result[len(q) :]


def shards(queries, key_rows, value_rows, out_grad):
    parts = lax.axis_size("head")
    rows = queries.shape[0]
    block = rows * parts
    heads = KV_HEADS // parts
    cores = 2 if heads % 2 == 0 else 1
    chunks = heads // cores
    ctx = lax.axis_index("ctx")
    place = jnp.stack(
        [lax.axis_index("head"), ctx // cores, ctx % cores, jnp.int32(cores)]
    ).astype(jnp.int32)

    kv_pieces = local_call(
        functools.partial(pack_two, parts, heads * HEAD_DIM, 1),
        [struct((rows, 2 * heads * HEAD_DIM))] * parts,
        (place, key_rows, value_rows),
    )
    kv_pieces = to_partners(kv_pieces, parts)
    q_piece = struct((rows, 2 * cores * Q_COLS))
    q_pieces = local_call(
        functools.partial(pack_two, parts, cores * Q_COLS, chunks),
        [q_piece] * (parts * chunks),
        (place, queries, out_grad),
    )
    arrived = [to_partners(q_pieces[c::chunks], parts) for c in range(chunks)]
    kv_split = local_call(
        functools.partial(split_rows, parts, chunks, HEAD_DIM),
        [struct((block, 2 * HEAD_DIM))] * (cores * chunks),
        (place, *kv_pieces),
    )
    halos = []
    for chunk in range(chunks):
        keep = kv_split[chunk]
        if cores == 2:
            give = kv_split[chunks + chunk]
            halos.append(
                (ctx_moved(keep, 2, 0), ctx_moved(give, 2, 1), keep, ctx_moved(give, 0, 1))
            )
        else:
            halos.append((ctx_moved(keep, 2, 0), ctx_moved(keep, 1, 0), keep))
    dq_back, kv_back = [], []
    for chunk in range(chunks):
        q_split = local_call(
            functools.partial(split_rows, parts, 1, Q_COLS),
            [struct((block, 2 * Q_COLS))] * cores,
            (place, *arrived[chunk]),
        )
        kv_piece = struct((rows, cores * 2 * HEAD_DIM))
        dq_piece = struct((rows, cores * Q_COLS))
        low, wide = jnp.bfloat16, jnp.float32
        if cores == 2:
            q_here = [q_split[0], ctx_moved(q_split[1], 0, 1)]
            (dq_keep, dq_give), (far_a, far_b, own, give) = attend_call(
                row_starts_pair, halos[chunk], q_here, (low, low, wide, low), place
            )
            dq_got = ctx_moved(dq_give, 0, 1)
            far_a = ctx_moved(far_a, -2, 0)
            far_b = ctx_moved(far_b, -2, 1)
            got = ctx_moved(give, 0, 1)
            dq_sent = local_call(
                functools.partial(cut_queries, parts), [dq_piece] * parts, (place, dq_keep, dq_got)
            )
            kv_sent = local_call(
                functools.partial(cut_keys, parts),
                [kv_piece] * parts,
                (place, own, far_a, got, far_b),
            )
        else:
            (dq_keep,), (far, near, own) = attend_call(
                row_starts_single, halos[chunk], q_split, (low, low, wide), place
            )
            far = ctx_moved(far, -2, 0)
            near = ctx_moved(near, -1, 0)
            sent = local_call(
                functools.partial(add_up, parts),
                [dq_piece] * parts + [kv_piece] * parts,
                (place, dq_keep, own, near, far),
            )
            dq_sent, kv_sent = sent[:parts], sent[parts:]
        dq_back.append(to_partners(dq_sent, parts))
        kv_back.append(to_partners(kv_sent, parts))
    (query_grad,) = local_call(
        functools.partial(unpack, parts, chunks, cores * Q_COLS),
        [struct(queries.shape)],
        (place, *[dq_back[c][s] for s in range(parts) for c in range(chunks)]),
    )
    key_grad, value_grad = local_call(
        functools.partial(unpack, parts, chunks, cores * HEAD_DIM),
        [struct(key_rows.shape), struct(value_rows.shape)],
        (place, *[kv_back[c][s] for s in range(parts) for c in range(chunks)]),
    )
    return query_grad, key_grad, value_grad


def solution(mesh):
    spec = P(("ctx", "head"), None)
    return jax.shard_map(
        shards,
        mesh=mesh,
        in_specs=(spec, spec, spec, spec),
        out_specs=(spec, spec, spec),
        check_vma=False,
    )
```

```python
import functools

import jax
import jax.numpy as jnp
from jax import lax
from jax.experimental import pallas as pl
from jax.experimental.pallas import tpu as pltpu
from jax.sharding import PartitionSpec as P


HEAD_DIM = 128
Q_HEADS = 32
KV_HEADS = 16
WINDOW = 1024
GROUPS = Q_HEADS // KV_HEADS
Q_COLS = GROUPS * HEAD_DIM
TILE = 128

score_scale = 168.0 ** (-0.5)
LOG2_E = 1.4426950408889634


def vmem():
    return pl.BlockSpec(memory_space=pltpu.VMEM)


def smem():
    return pl.BlockSpec(memory_space=pltpu.SMEM)


def moved_bytes(arrays):
    return sum(a.size * a.dtype.itemsize for a in arrays)


def local_call(body, outs, args, flops=0, transcendentals=0, scratch=()):
    return pl.pallas_call(
        body,
        out_shape=outs,
        in_specs=[smem()] + [vmem()] * (len(args) - 1),
        out_specs=[vmem()] * len(outs),
        scratch_shapes=list(scratch),
        cost_estimate=pl.CostEstimate(
            flops=flops,
            transcendentals=transcendentals,
            bytes_accessed=moved_bytes(list(args[1:]) + list(outs)),
        ),
    )(*args)


def sent_to(place, step, parts):
    if parts == 4 and step in (1, 3):
        return lax.rem(2 * place + 1 if step == 1 else 3 * place + 2, 5)
    if parts == 4 and step == 2:
        step = 3
    return jnp.bitwise_xor(place, step)


def came_from(place, step, parts):
    return sent_to(place, (parts - step) % parts if parts == 4 else step, parts)


def across(shard, parts, step):
    if parts == 4:
        moves = list(enumerate({1: (1, 3, 0, 2), 2: (3, 2, 1, 0), 3: (2, 0, 3, 1)}[step]))
    else:
        moves = [(i, i ^ step) for i in range(parts)]
    return lax.ppermute(shard, "head", moves)


def pack_two(parts, width, chunks, place, left, right, *outs):
    for step in range(parts):
        partner = sent_to(place[0], step, parts)
        for chunk in range(chunks):
            out = outs[step * chunks + chunk]
            start = pl.multiple_of((partner * chunks + chunk) * width, width)
            out[:, 0:width] = left[:, pl.ds(start, width)]
            out[:, width : 2 * width] = right[:, pl.ds(start, width)]


def split_rows(parts, pairs, width, place, *refs):
    outs = refs[parts:]
    rows = refs[0].shape[0]
    for step in range(parts):
        partner = came_from(place[0], step, parts)
        at = pl.ds(pl.multiple_of(partner * rows, rows), rows)
        for pair in range(pairs):
            for other in range(len(outs) // pairs):
                core = jnp.bitwise_xor(place[2], other)
                for side in range(2):
                    start = ((side * pairs + pair) * place[3] + core) * width
                    outs[other * pairs + pair][at, side * width : (side + 1) * width] = refs[step][
                        :, pl.ds(pl.multiple_of(start, width), width)
                    ]


def attend(kv_count, q_count, starts, place, *refs):
    kv_refs = refs[:kv_count]
    q_refs = refs[kv_count : kv_count + q_count]
    dq_outs = refs[kv_count + q_count : kv_count + 2 * q_count]
    kv_outs = refs[kv_count + 2 * q_count : 2 * kv_count + 2 * q_count]
    scratch = refs[2 * kv_count + 2 * q_count :]
    q_rows, g_rows, keys, values, keys_t, score, att_low, d_low, dk, dv, dq_all = scratch
    block = q_refs[0].shape[0]
    span = score.shape[0]
    tiles = span // TILE
    places = [pl.ds(pl.multiple_of(at, TILE), block) for at in starts(place, block)]
    for at, q in zip(places[kv_count:], q_refs):
        q_rows[at, :] = q[:, 0:Q_COLS]
        g_rows[at, :] = q[:, Q_COLS : 2 * Q_COLS]
    for at, kv in zip(places, kv_refs):
        keys[at, :] = kv[:, 0:HEAD_DIM]
        values[at, :] = kv[:, HEAD_DIM : 2 * HEAD_DIM]
        keys_t[:, at] = kv[:, 0:HEAD_DIM].T
    dk[...] = jnp.zeros_like(dk)
    dv[...] = jnp.zeros_like(dv)
    first_key = WINDOW - place[1] * (q_count * block)
    lanes = GROUPS * TILE
    key_id = lax.broadcasted_iota(jnp.int32, (TILE, lanes), 0)
    row_id = jnp.bitwise_and(lax.broadcasted_iota(jnp.int32, (TILE, lanes), 1), TILE - 1)
    lower = key_id <= row_id
    exponent = jnp.float32(score_scale * LOG2_E)

    def fold(x):
        return x.reshape(TILE // 8, 8, lanes)

    for row_block in range(q_count * block // TILE):
        base = row_block * TILE
        these = slice(base, base + TILE)
        q_two = jnp.concatenate(
            [q_rows[these, g * HEAD_DIM : (g + 1) * HEAD_DIM] for g in range(GROUPS)], axis=0
        )
        g_two = jnp.concatenate(
            [g_rows[these, g * HEAD_DIM : (g + 1) * HEAD_DIM] for g in range(GROUPS)], axis=0
        )
        there = slice(base, base + span)
        q_t, g_t = q_two.T, g_two.T

        def scores(t):
            s = jnp.dot(
                keys[base + t * TILE : base + (t + 1) * TILE, :],
                q_t,
                preferred_element_type=jnp.float32,
            )
            if t == 0:
                s = jnp.where(lower, -1e30, s)
            if t == tiles - 1:
                s = jnp.where(lower, s, -1e30)
            return s

        def d_attention(t):
            return jnp.dot(
                values[base + t * TILE : base + (t + 1) * TILE, :],
                g_t,
                preferred_element_type=jnp.float32,
            )

        top = jnp.full((8, lanes), -1e30, jnp.float32)
        for t in range(tiles):
            gone = jnp.where(base + t * TILE < first_key, -1e30, 0.0)
            top = jnp.maximum(top, jnp.max(fold(scores(t)), axis=0) + gone)
        top = jnp.max(top, axis=0, keepdims=True)
        total = jnp.zeros((8, lanes), jnp.float32)
        inner = jnp.zeros((8, lanes), jnp.float32)
        for t in range(tiles):
            here = slice(t * TILE, (t + 1) * TILE)
            level = top + jnp.where(base + t * TILE < first_key, 1e30, 0.0)
            p = jnp.exp2((scores(t) - level) * exponent)
            score[here, :] = p
            total = total + jnp.sum(fold(p), axis=0)
            inner = inner + jnp.sum(fold(p * d_attention(t)), axis=0)
        inverse = 1.0 / jnp.sum(total, axis=0, keepdims=True)
        center = jnp.sum(inner, axis=0, keepdims=True) * inverse
        for t in range(tiles):
            here = slice(t * TILE, (t + 1) * TILE)
            att = score[here, :] * inverse
            att_low[here, :] = att.astype(jnp.bfloat16)
            d_low[here, :] = (att * (d_attention(t) - center)).astype(jnp.bfloat16)
        dv[there, :] += jnp.dot(att_low[...], g_two, preferred_element_type=jnp.float32)
        dk[there, :] += jnp.dot(d_low[...], q_two, preferred_element_type=jnp.float32)
        dq_t = jnp.dot(keys_t[:, there], d_low[...], preferred_element_type=jnp.float32)
        dq = (dq_t * score_scale).T.astype(jnp.bfloat16)
        for g in range(GROUPS):
            dq_all[these, g * HEAD_DIM : (g + 1) * HEAD_DIM] = dq[g * TILE : (g + 1) * TILE, :]
    for at, out in zip(places[kv_count:], dq_outs):
        out[...] = dq_all[at, :]
    for at, out in zip(places, kv_outs):
        out[:, 0:HEAD_DIM] = (dk[at, :] * score_scale).astype(out.dtype)
        out[:, HEAD_DIM : 2 * HEAD_DIM] = dv[at, :].astype(out.dtype)


def row_starts_single(place, block):
    return [0, block, 2 * block, 0]


def row_starts_pair(place, block):
    here, there = place[2] * block, (1 - place[2]) * block
    return [here, there, 2 * block + here, 2 * block + there, here, there]


def cut_queries(parts, place, kept, given, *outs):
    rows = outs[0].shape[0]
    width = kept.shape[1]
    for step in range(parts):
        at = pl.ds(pl.multiple_of(sent_to(place[0], step, parts) * rows, rows), rows)
        for other, source in enumerate((kept, given)):
            core = jnp.bitwise_xor(place[2], other)
            outs[step][:, pl.ds(pl.multiple_of(core * width, width), width)] = source[at, :]


def cut_keys(parts, place, own, own_far, given, given_far, *outs):
    rows = outs[0].shape[0]
    for step in range(parts):
        at = pl.ds(pl.multiple_of(sent_to(place[0], step, parts) * rows, rows), rows)
        for other, (one, two) in enumerate(((own, own_far), (given, given_far))):
            core = jnp.bitwise_xor(place[2], other)
            total = (one[at, :].astype(jnp.float32) + two[at, :].astype(jnp.float32)).astype(
                jnp.bfloat16
            )
            for side in range(2):
                start = pl.multiple_of((2 * side + core) * HEAD_DIM, HEAD_DIM)
                outs[step][:, pl.ds(start, HEAD_DIM)] = total[
                    :, side * HEAD_DIM : (side + 1) * HEAD_DIM
                ]


def add_up(parts, place, dq, own, near, far, *outs):
    rows = outs[0].shape[0]
    for step in range(parts):
        partner = sent_to(place[0], step, parts)
        at = pl.ds(pl.multiple_of(partner * rows, rows), rows)
        outs[step][:, 0:Q_COLS] = dq[at, :]
        total = own[at, :] + near[at, :].astype(jnp.float32) + far[at, :].astype(jnp.float32)
        outs[parts + step][:, 0 : 2 * HEAD_DIM] = total.astype(jnp.bfloat16)


def unpack(parts, chunks, width, place, *refs):
    pieces = refs[: parts * chunks]
    outs = refs[parts * chunks :]
    for step in range(parts):
        partner = came_from(place[0], step, parts)
        for chunk in range(chunks):
            piece = pieces[step * chunks + chunk]
            start = pl.multiple_of((partner * chunks + chunk) * width, width)
            for i, out in enumerate(outs):
                out[:, pl.ds(start, width)] = piece[:, i * width : (i + 1) * width]


def struct(shape, dtype=jnp.bfloat16):
    return jax.ShapeDtypeStruct(shape, dtype)


def to_partners(pieces, parts):
    return [pieces[0]] + [across(pieces[s], parts, s) for s in range(1, parts)]


def ctx_moved(shard, by, flip):
    count = lax.axis_size("ctx")
    moves = [(i, (i + by) ^ flip) for i in range(count) if 0 <= i + by < count]
    return lax.ppermute(shard, "ctx", moves)


def attend_call(starts, kv, q, kv_dtypes, place):
    block = q[0].shape[0]
    rows, key_count, span = len(q) * block, len(kv) * block, WINDOW + TILE
    lanes = GROUPS * TILE
    pairs = rows * span * GROUPS
    low, wide = jnp.bfloat16, jnp.float32
    outs = [struct((block, Q_COLS))] * len(q) + [
        struct((block, 2 * HEAD_DIM), dtype) for dtype in kv_dtypes
    ]
    result = functools.partial(
        local_call,
        flops=10 * pairs * HEAD_DIM,
        transcendentals=pairs,
        scratch=[
            pltpu.VMEM((rows, Q_COLS), low),
            pltpu.VMEM((rows, Q_COLS), low),
            pltpu.VMEM((key_count, HEAD_DIM), low),
            pltpu.VMEM((key_count, HEAD_DIM), low),
            pltpu.VMEM((HEAD_DIM, key_count), low),
            pltpu.VMEM((span, lanes), wide),
            pltpu.VMEM((span, lanes), low),
            pltpu.VMEM((span, lanes), low),
            pltpu.VMEM((key_count, HEAD_DIM), wide),
            pltpu.VMEM((key_count, HEAD_DIM), wide),
            pltpu.VMEM((rows, Q_COLS), low),
        ],
    )(functools.partial(attend, len(kv), len(q), starts), outs, (place, *kv, *q))
    return result[: len(q)], result[len(q) :]


def shards(queries, key_rows, value_rows, out_grad):
    parts = lax.axis_size("head")
    rows = queries.shape[0]
    block = rows * parts
    heads = KV_HEADS // parts
    cores = 2 if heads % 2 == 0 else 1
    chunks = heads // cores
    ctx = lax.axis_index("ctx")
    place = jnp.stack(
        [lax.axis_index("head"), ctx // cores, ctx % cores, jnp.int32(cores)]
    ).astype(jnp.int32)

    kv_pieces = local_call(
        functools.partial(pack_two, parts, heads * HEAD_DIM, 1),
        [struct((rows, 2 * heads * HEAD_DIM))] * parts,
        (place, key_rows, value_rows),
    )
    kv_pieces = to_partners(kv_pieces, parts)
    q_piece = struct((rows, 2 * cores * Q_COLS))
    q_pieces = local_call(
        functools.partial(pack_two, parts, cores * Q_COLS, chunks),
        [q_piece] * (parts * chunks),
        (place, queries, out_grad),
    )
    arrived = [to_partners(q_pieces[c::chunks], parts) for c in range(chunks)]
    kv_split = local_call(
        functools.partial(split_rows, parts, chunks, HEAD_DIM),
        [struct((block, 2 * HEAD_DIM))] * (cores * chunks),
        (place, *kv_pieces),
    )
    halos = []
    for chunk in range(chunks):
        keep = kv_split[chunk]
        if cores == 2:
            give = kv_split[chunks + chunk]
            halos.append(
                (ctx_moved(keep, 2, 0), ctx_moved(give, 2, 1), keep, ctx_moved(give, 0, 1))
            )
        else:
            halos.append((ctx_moved(keep, 2, 0), ctx_moved(keep, 1, 0), keep))
    dq_back, kv_back = [], []
    for chunk in range(chunks):
        q_split = local_call(
            functools.partial(split_rows, parts, 1, Q_COLS),
            [struct((block, 2 * Q_COLS))] * cores,
            (place, *arrived[chunk]),
        )
        kv_piece = struct((rows, cores * 2 * HEAD_DIM))
        dq_piece = struct((rows, cores * Q_COLS))
        low, wide = jnp.bfloat16, jnp.float32
        if cores == 2:
            q_here = [q_split[0], ctx_moved(q_split[1], 0, 1)]
            (dq_keep, dq_give), (far_a, far_b, own, give) = attend_call(
                row_starts_pair, halos[chunk], q_here, (low, low, wide, low), place
            )
            dq_got = ctx_moved(dq_give, 0, 1)
            far_a = ctx_moved(far_a, -2, 0)
            far_b = ctx_moved(far_b, -2, 1)
            got = ctx_moved(give, 0, 1)
            dq_sent = local_call(
                functools.partial(cut_queries, parts), [dq_piece] * parts, (place, dq_keep, dq_got)
            )
            kv_sent = local_call(
                functools.partial(cut_keys, parts),
                [kv_piece] * parts,
                (place, own, far_a, got, far_b),
            )
        else:
            (dq_keep,), (far, near, own) = attend_call(
                row_starts_single, halos[chunk], q_split, (low, low, wide), place
            )
            far = ctx_moved(far, -2, 0)
            near = ctx_moved(near, -1, 0)
            sent = local_call(
                functools.partial(add_up, parts),
                [dq_piece] * parts + [kv_piece] * parts,
                (place, dq_keep, own, near, far),
            )
            dq_sent, kv_sent = sent[:parts], sent[parts:]
        dq_back.append(to_partners(dq_sent, parts))
        kv_back.append(to_partners(kv_sent, parts))
    (query_grad,) = local_call(
        functools.partial(unpack, parts, chunks, cores * Q_COLS),
        [struct(queries.shape)],
        (place, *[dq_back[c][s] for s in range(parts) for c in range(chunks)]),
    )
    key_grad, value_grad = local_call(
        functools.partial(unpack, parts, chunks, cores * HEAD_DIM),
        [struct(key_rows.shape), struct(value_rows.shape)],
        (place, *[kv_back[c][s] for s in range(parts) for c in range(chunks)]),
    )
    return query_grad, key_grad, value_grad


def solution(mesh):
    spec = P(("ctx", "head"), None)
    return jax.shard_map(
        shards,
        mesh=mesh,
        in_specs=(spec, spec, spec, spec),
        out_specs=(spec, spec, spec),
        check_vma=False,
    )
```
